256 devices in a mesh: dom: 32 (over x, z), grp: 8 (over y, core).
Axes of the slice: x: 4, y: 4, z: 8, core: 2. Of those that a mesh axis runs over, the one named last changes fastest.
Arguments:
- node_feats: bfloat16 [65536, 1024], P(('dom', 'grp')), may hold values from -6 to 6
- weight: bfloat16 [1024, 512], replicated, may hold values from -0.1875 to 0.1875
- bias: float32 [512], replicated, may hold values from -4 to 4
- cotangent: bfloat16 [65536, 512], P(('dom', 'grp')), may hold values from -6 to 6
- tile_bank: bfloat16 [16, 128, 128], replicated, may hold values from -0.125 to 0.125
- local_cols: int32 [32, 16, 16], P('dom'), may hold values from 0 to 15
- local_banks: int32 [32, 16, 16], P('dom'), may hold values from 0 to 15
- published: int32 [32, 4], P('dom'), may hold values from 0 to 15, as said below
- send_table: int32 [32, 32, 2], replicated, may hold values from -1 to 3, as said below
- halo_rows: int32 [32, 32, 2], P('dom'), may hold values from 0 to 15
- halo_banks: int32 [32, 32, 2], P('dom'), may hold values from 0 to 15
Outputs:
- activations: bfloat16 [65536, 512], P(('dom', 'grp'))
- grad_nodes: bfloat16 [65536, 1024], P(('dom', 'grp'))
- grad_weight: float32 [1024, 512], replicated
- grad_bias: float32 [512], replicated
The draws below stay inside these ranges and needn't reach their ends.
Inputs may be any that keep to these rules, and one draw needn't show every extreme that they name: `published`: the 4 entries of a partition are distinct block numbers of that partition; 0 and 15 each appear in some partition's list. `send_table`: entry s of the pair (src, p) is -1 or an index into the offered list of src; the live entries of a pair come first and are distinct; a pair (p, p) has none; some pair has all 2 entries live.
All inputs are finite; a program needn't handle non-finite values.
Results may differ from the reference program's by a relative error of at most 0.019.
The reference program's roundings to bfloat16 on the way (of `aggregated`, `grad_pre` and `grad_agg`) count: a program that leaves them out, or rounds other values in their place, can miss the bound.
Values may be sent and summed in bfloat16 or wider, within the bound.
A program may use at most 64 MiB of HBM per device.

```python
import jax
import jax.numpy as jnp
from jax import lax

EMBED = 1024
HIDDEN_SIZE = 512
TILE = 128
LOCAL_TILES = 16
BANK_TILES = 16
PUB_BLOCKS = 4
SLOTS = 2
DOMAINS = 32
BLOCKS = 16
NODES = 65536


def draw_published(key, part):
    key_perm, key_pick = jax.random.split(key, 2)
    part_keys = jax.random.split(key_perm, DOMAINS)

    def offered(single):
        return jax.random.permutation(single, BLOCKS)[:PUB_BLOCKS]
    lists = jax.vmap(offered)(part_keys).astype(jnp.int32)
    chosen = jax.random.randint(key_pick, (), 0, DOMAINS)
    after = (chosen + 1) % DOMAINS
    domain_ids = jnp.arange(DOMAINS)[:, None]
    shift_top = (BLOCKS - 1 - lists[:, :1]) % BLOCKS
    shift_low = (BLOCKS - lists[:, :1]) % BLOCKS
    shifts = jnp.where(domain_ids == chosen, shift_top, jnp.where(domain_ids == after, shift_low, 0))
    return ((lists + shifts) % BLOCKS).astype(jnp.int32)


def draw_send_table(key, part):
    key_heavy, key_light, key_offset, key_pick = jax.random.split(key, 4)
    source = jnp.arange(DOMAINS)[:, None]
    target = jnp.arange(DOMAINS)[None, :]
    chosen = jax.random.randint(key_pick, (), 0, DOMAINS)
    heavy_rows = jax.random.randint(key_heavy, (DOMAINS, 1), 0, 2)
    heavy_rows = jnp.maximum(heavy_rows, (source == chosen).astype(jnp.int32))
    light_counts = jax.random.randint(key_light, (DOMAINS, DOMAINS), 0, SLOTS)
    counts = jnp.where(heavy_rows > 0, SLOTS, light_counts)
    counts = jnp.where(source == target, 0, counts)
    offsets = jax.random.randint(key_offset, (DOMAINS, DOMAINS), 0, PUB_BLOCKS)
    forced = (source == chosen) & (target == (chosen + 1) % DOMAINS)
    offsets = jnp.where(forced, PUB_BLOCKS - 1, offsets)
    slot_index = jnp.arange(SLOTS)[None, None, :]
    pair_table = (offsets[:, :, None] + slot_index) % PUB_BLOCKS
    return jnp.where(slot_index < counts[:, :, None], pair_table, -1).astype(jnp.int32)


def plant(array, stream_key, low, high):
    longest = array.shape.index(max(array.shape))
    spots = []
    for shift in (0, 1):
        where = [jax.random.randint(jax.random.fold_in(stream_key, axis), (), 0, length) for axis, length in enumerate(array.shape)]
        where[longest] = (where[longest] + shift) % array.shape[longest]
        spots.append(tuple(where))
    return array.at[spots[0]].set(low).at[spots[1]].set(high)


def levels(rng, extent, cuts, low, largest):
    level, own = 1.0, jax.random.fold_in(rng, 6)
    for dim, shards_of in cuts:
        steps = jnp.exp(jax.random.uniform(jax.random.fold_in(own, dim), (shards_of,), jnp.float32, low / len(cuts), largest / len(cuts)))
        level = level * jnp.repeat(steps, extent[dim] // shards_of).reshape([-1 if axis == dim else 1 for axis in range(len(extent))])
    return level


def scatter_about(rng, extent, spread, most, cuts=(), kind=jnp.bfloat16):
    entries = spread * jax.random.normal(rng, extent, jnp.float32)
    if cuts:
        entries = entries * levels(rng, extent, cuts, -0.22, 0.18)
    return jnp.clip(entries, -most, most).astype(kind)


def setup_inputs(seed: int = 0) -> dict:
    key_of = jax.random.split(jax.random.key(seed), 12)
    return {
        "node_feats": scatter_about(key_of[0], (NODES, EMBED), 1.0, 6.0, ((0, 256),)),
        "weight": scatter_about(key_of[1], (EMBED, HIDDEN_SIZE), EMBED ** -0.5, 0.1875),
        "bias": scatter_about(key_of[2], (HIDDEN_SIZE,), 1.0, 4.0, (), jnp.float32),
        "cotangent": scatter_about(key_of[3], (NODES, HIDDEN_SIZE), 1.0, 6.0, ((0, 256),)),
        "tile_bank": scatter_about(key_of[4], (BANK_TILES, TILE, TILE), (TILE * (LOCAL_TILES + 2)) ** -0.5, 0.125),
        "local_cols": plant(jax.random.randint(key_of[5], (DOMAINS, BLOCKS, LOCAL_TILES), 0, BLOCKS), jax.random.fold_in(key_of[5], 1), 0, BLOCKS - 1).astype(jnp.int32),
        "local_banks": plant(jax.random.randint(key_of[6], (DOMAINS, BLOCKS, LOCAL_TILES), 0, BANK_TILES), jax.random.fold_in(key_of[6], 1), 0, BANK_TILES - 1).astype(jnp.int32),
        "published": draw_published(jax.random.fold_in(key_of[11], 71), 0),
        "send_table": draw_send_table(jax.random.fold_in(key_of[11], 71), 0),
        "halo_rows": plant(jax.random.randint(key_of[9], (DOMAINS, DOMAINS, SLOTS), 0, BLOCKS), jax.random.fold_in(key_of[9], 1), 0, BLOCKS - 1).astype(jnp.int32),
        "halo_banks": plant(jax.random.randint(key_of[10], (DOMAINS, DOMAINS, SLOTS), 0, BANK_TILES), jax.random.fold_in(key_of[10], 1), 0, BANK_TILES - 1).astype(jnp.int32),
    }


def block_view(whole):
    return whole.reshape(DOMAINS, BLOCKS, TILE, whole.shape[1])


def reference(node_feats, weight, bias, cotangent, tile_bank, local_cols, local_banks, published, send_table, halo_rows, halo_banks):
    feat_blocks = block_view(node_feats)
    bank_wide = tile_bank.astype(jnp.float32)
    embed_width = node_feats.shape[1]
    sources = jnp.broadcast_to(jnp.arange(DOMAINS, dtype=jnp.int32)[:, None], (DOMAINS, SLOTS))
    domain_ids = jnp.arange(DOMAINS, dtype=jnp.int32)

    def forward_part(domain):
        own_blocks = feat_blocks[domain].astype(jnp.float32)
        cols_here = local_cols[domain]
        banks_here = local_banks[domain]

        def add_tiles(position, running):
            column = lax.dynamic_index_in_dim(cols_here, position, 1, keepdims=False)
            bank_ids = lax.dynamic_index_in_dim(banks_here, position, 1, keepdims=False)
            return running + jnp.einsum("rij,rjf->rif", bank_wide[bank_ids], own_blocks[column])

        running = lax.fori_loop(0, LOCAL_TILES, add_tiles, jnp.zeros((BLOCKS, TILE, embed_width), jnp.float32))
        incoming = send_table[:, domain, :]
        live_in = (incoming >= 0).astype(jnp.float32)[:, :, None, None]
        block_ids = published[sources, jnp.maximum(incoming, 0)]
        remote = feat_blocks[sources, block_ids].astype(jnp.float32)
        halo_terms = jnp.einsum("dsij,dsjf->dsif", bank_wide[halo_banks[domain]], remote) * live_in
        running = running + jax.ops.segment_sum(halo_terms.reshape(DOMAINS * SLOTS, TILE, embed_width), halo_rows[domain].reshape(-1), num_segments=BLOCKS)
        return running.astype(jnp.bfloat16)

    aggregated = lax.map(forward_part, domain_ids).reshape(NODES, embed_width)
    pre_act = jnp.dot(aggregated, weight, preferred_element_type=jnp.float32) + bias.astype(jnp.float32)
    activations = jnp.maximum(pre_act, 0.0).astype(jnp.bfloat16)
    grad_pre = jnp.where(pre_act > 0, cotangent.astype(jnp.float32), 0.0).astype(jnp.bfloat16)
    norm_scale = NODES ** -0.5
    grad_weight = jnp.dot(aggregated.T, grad_pre, preferred_element_type=jnp.float32) * norm_scale
    grad_bias = jnp.sum(grad_pre.astype(jnp.float32), axis=0) * norm_scale
    grad_agg = jnp.dot(grad_pre, weight.T, preferred_element_type=jnp.float32).astype(jnp.bfloat16)
    grad_blocks = block_view(grad_agg)

    def backward_part(domain):
        own_grads = grad_blocks[domain].astype(jnp.float32)
        cols_here = local_cols[domain]
        banks_here = local_banks[domain]

        def add_tiles(position, running):
            column = lax.dynamic_index_in_dim(cols_here, position, 1, keepdims=False)
            bank_ids = lax.dynamic_index_in_dim(banks_here, position, 1, keepdims=False)
            contrib = jnp.einsum("rji,rjf->rif", bank_wide[bank_ids], own_grads)
            return running + jax.ops.segment_sum(contrib, column, num_segments=BLOCKS)

        running = lax.fori_loop(0, LOCAL_TILES, add_tiles, jnp.zeros((BLOCKS, TILE, embed_width), jnp.float32))
        outgoing = send_table[domain]
        live_out = (outgoing >= 0).astype(jnp.float32)[:, :, None, None]
        targets = jnp.where(outgoing >= 0, published[domain][jnp.maximum(outgoing, 0)], BLOCKS).astype(jnp.int32)
        reader_rows = halo_rows[:, domain, :]
        reader_banks = halo_banks[:, domain, :]
        read_grads = grad_blocks[sources, reader_rows].astype(jnp.float32)
        back_terms = jnp.einsum("dsji,dsjf->dsif", bank_wide[reader_banks], read_grads) * live_out
        back_total = jax.ops.segment_sum(back_terms.reshape(DOMAINS * SLOTS, TILE, embed_width), targets.reshape(-1), num_segments=BLOCKS + 1)
        running = running + back_total[:BLOCKS]
        return running.astype(jnp.bfloat16)

    grad_nodes = lax.map(backward_part, domain_ids).reshape(NODES, embed_width)
    return activations, grad_nodes, grad_weight, grad_bias
```

```python
import functools

import jax
import jax.numpy as jnp
from jax import lax
from jax.experimental import pallas as pl
from jax.experimental.pallas import tpu as pltpu
from jax.sharding import PartitionSpec as P

_SMEM = pl.BlockSpec(memory_space=pltpu.SMEM)
_VMEM = pl.BlockSpec(memory_space=pltpu.VMEM)


def _cost(matmuls, tile, nbytes):
    return pl.CostEstimate(
        flops=2 * matmuls * tile * tile * tile, transcendentals=0, bytes_accessed=nbytes
    )


def _fwd_local_kernel(cols, banks, bank_ref, feat_ref, acc_ref):
    rows, tiles = cols.shape

    def row(r, carry):
        total = jnp.zeros(acc_ref.shape[1:], jnp.float32)
        for k in range(tiles):
            total += jnp.dot(
                bank_ref[banks[r, k]], feat_ref[cols[r, k]], preferred_element_type=jnp.float32
            )
        acc_ref[r] = total
        return carry

    lax.fori_loop(0, rows, row, 0)


def _bwd_local_kernel(cols, banks, bank_t_ref, grad_ref, acc_ref):
    rows, tiles = cols.shape
    acc_ref[...] = jnp.zeros(acc_ref.shape, jnp.float32)

    def row(r, carry):
        block = grad_ref[r]
        for k in range(tiles):
            c = cols[r, k]
            acc_ref[c] += jnp.dot(
                bank_t_ref[banks[r, k]], block, preferred_element_type=jnp.float32
            )
        return carry

    lax.fori_loop(0, rows, row, 0)


def _halo_kernel(dest, banks, live, bank_ref, acc_in, blocks_ref, out_ref, acc_ref):
    acc_ref[...] = acc_in[...]

    def term(j, carry):
        @pl.when(live[j] > 0)
        def _():
            acc_ref[dest[j]] += jnp.dot(
                bank_ref[banks[j]], blocks_ref[j], preferred_element_type=jnp.float32
            )

        return carry

    lax.fori_loop(0, dest.shape[0], term, 0)
    out_ref[...] = acc_ref[...].astype(out_ref.dtype)


def _local(kernel, cols, banks, bank, blocks):
    n, tile, width = blocks.shape
    return pl.pallas_call(
        kernel,
        out_shape=jax.ShapeDtypeStruct((n, tile, width), jnp.float32),
        in_specs=[_SMEM, _SMEM, _VMEM, _VMEM],
        out_specs=_VMEM,
        cost_estimate=_cost(cols.size, tile, 2 * bank.size + 2 * blocks.size + 4 * blocks.size),
    )(cols, banks, bank, blocks)


def _halo(dest, banks, live, bank, acc, blocks):
    n, tile, width = acc.shape
    return pl.pallas_call(
        _halo_kernel,
        out_shape=jax.ShapeDtypeStruct((n, tile, width), jnp.bfloat16),
        in_specs=[_SMEM, _SMEM, _SMEM, _VMEM, _VMEM, _VMEM],
        out_specs=_VMEM,
        scratch_shapes=[pltpu.VMEM((n, tile, width), jnp.float32)],
        cost_estimate=_cost(dest.size, tile, 2 * bank.size + 6 * acc.size + 2 * blocks.size),
    )(dest, banks, live, bank, acc, blocks)


def _all_reduce(x):
    groups = lax.axis_size("grp")
    domains = lax.axis_size("dom")
    rows, width = x.shape
    chunk = -(-rows // groups)
    x = jnp.pad(x, ((0, chunk * groups - rows), (0, 0)))
    y = lax.all_to_all(x.reshape(groups, chunk, width), "grp", 0, 0, tiled=True).sum(0)
    piece = -(-chunk // domains)
    y = jnp.pad(y, ((0, piece * domains - chunk), (0, 0)))
    z = lax.all_to_all(y.reshape(domains, piece, width), "dom", 0, 0, tiled=True).sum(0)
    z = lax.all_to_all(
        jnp.broadcast_to(z[None], (domains, piece, width)), "dom", 0, 0, tiled=True
    ).reshape(domains * piece, width)[:chunk]
    z = lax.all_to_all(
        jnp.broadcast_to(z[None], (groups, chunk, width)), "grp", 0, 0, tiled=True
    ).reshape(groups * chunk, width)
    return z[:rows]


def per_device(
    node_feats,
    weight,
    bias,
    cotangent,
    tile_bank,
    local_cols,
    local_banks,
    published,
    send_table,
    halo_rows,
    halo_banks,
):
    domains = lax.axis_size("dom")
    groups = lax.axis_size("grp")
    domain_index = lax.axis_index("dom")
    rows_here = node_feats.shape[0]
    tile_size = tile_bank.shape[1]
    slot_count = send_table.shape[2]
    features = lax.all_to_all(node_feats, "grp", split_axis=1, concat_axis=0, tiled=True)
    part_rows, narrow = features.shape
    blocks = part_rows // tile_size
    feat_blocks = features.reshape(blocks, tile_size, narrow)
    cols_here = local_cols[0]
    banks_here = local_banks[0]
    own_pub = published[0]
    bank_t = jnp.swapaxes(tile_bank, 1, 2)

    outgoing = lax.dynamic_index_in_dim(send_table, domain_index, 0, keepdims=False)
    send_ids = own_pub[jnp.maximum(outgoing, 0)]
    remote = lax.all_to_all(feat_blocks[send_ids], "dom", 0, 0, tiled=True)
    incoming = lax.dynamic_index_in_dim(send_table, domain_index, 1, keepdims=False)
    live_in = (incoming >= 0).astype(jnp.int32).reshape(-1)
    rows_in = halo_rows[0]

    local_acc = _local(_fwd_local_kernel, cols_here, banks_here, tile_bank, feat_blocks)
    agg_blocks = _halo(
        rows_in.reshape(-1),
        halo_banks[0].reshape(-1),
        live_in,
        tile_bank,
        local_acc,
        remote.reshape(domains * slot_count, tile_size, narrow),
    )
    agg_narrow = agg_blocks.reshape(part_rows, narrow)
    aggregated = lax.all_to_all(agg_narrow, "grp", split_axis=0, concat_axis=1, tiled=True)
    pre_act = jnp.dot(aggregated, weight, preferred_element_type=jnp.float32) + bias
    activations = jnp.maximum(pre_act, 0.0).astype(jnp.bfloat16)
    grad_pre = jnp.where(pre_act > 0, cotangent.astype(jnp.float32), 0.0).astype(jnp.bfloat16)
    weight_part = lax.dot_general(
        aggregated, grad_pre, (((0,), (0,)), ((), ())), preferred_element_type=jnp.float32
    )
    bias_part = jnp.sum(grad_pre.astype(jnp.float32), axis=0)
    grad_agg = lax.dot_general(
        grad_pre, weight, (((1,), (1,)), ((), ())), preferred_element_type=jnp.float32
    ).astype(jnp.bfloat16)
    grad_narrow = lax.all_to_all(grad_agg, "grp", split_axis=1, concat_axis=0, tiled=True)
    grad_blocks = grad_narrow.reshape(blocks, tile_size, narrow)

    back_in = lax.all_to_all(grad_blocks[rows_in], "dom", 0, 0, tiled=True)
    banks_back = lax.all_to_all(halo_banks[0], "dom", 0, 0, tiled=True)
    live_out = (outgoing >= 0).astype(jnp.int32).reshape(-1)

    local_back = _local(_bwd_local_kernel, cols_here, banks_here, bank_t, grad_blocks)
    grad_total = _halo(
        send_ids.reshape(-1),
        banks_back.reshape(-1),
        live_out,
        bank_t,
        local_back,
        back_in.reshape(domains * slot_count, tile_size, narrow),
    )
    grad_nodes = lax.all_to_all(
        grad_total.reshape(part_rows, narrow),
        "grp",
        split_axis=0,
        concat_axis=1,
        tiled=True,
    )
    norm_scale = float(rows_here * groups * domains) ** (-0.5)
    hidden = weight_part.shape[0]
    summed = _all_reduce(jnp.concatenate([weight_part, bias_part[None]], axis=0))
    return (
        activations,
        grad_nodes,
        summed[:hidden] * norm_scale,
        summed[hidden] * norm_scale,
    )


def solution(mesh):
    in_specs = (
        P(("dom", "grp"), None),
        P(),
        P(),
        P(("dom", "grp"), None),
        P(),
        P("dom", None, None),
        P("dom", None, None),
        P("dom", None),
        P(),
        P("dom", None, None),
        P("dom", None, None),
    )
    out_specs = (P(("dom", "grp"), None), P(("dom", "grp"), None), P(), P())
    return jax.shard_map(
        per_device, mesh=mesh, in_specs=in_specs, out_specs=out_specs, check_vma=False
    )
```

```python
import functools

import jax
import jax.numpy as jnp
from jax import lax
from jax.experimental import pallas as pl
from jax.experimental.pallas import tpu as pltpu
from jax.sharding import PartitionSpec as P

_SMEM = pl.BlockSpec(memory_space=pltpu.SMEM)
_VMEM = pl.BlockSpec(memory_space=pltpu.VMEM)


def _cost(matmuls, tile, nbytes):
    return pl.CostEstimate(
        flops=2 * matmuls * tile * tile * tile, transcendentals=0, bytes_accessed=nbytes
    )


def _fwd_local_kernel(cols, banks, bank_ref, feat_ref, acc_ref):
    rows, tiles = cols.shape

    def row(r, carry):
        total = jnp.zeros(acc_ref.shape[1:], jnp.float32)
        for k in range(tiles):
            total += jnp.dot(
                bank_ref[banks[r, k]], feat_ref[cols[r, k]], preferred_element_type=jnp.float32
            )
        acc_ref[r] = total
        return carry

    lax.fori_loop(0, rows, row, 0)


def _bwd_local_kernel(cols, banks, bank_t_ref, grad_ref, acc_ref):
    rows, tiles = cols.shape
    acc_ref[...] = jnp.zeros(acc_ref.shape, jnp.float32)

    def row(r, carry):
        block = grad_ref[r]
        for k in range(tiles):
            c = cols[r, k]
            acc_ref[c] += jnp.dot(
                bank_t_ref[banks[r, k]], block, preferred_element_type=jnp.float32
            )
        return carry

    lax.fori_loop(0, rows, row, 0)


def _halo_kernel(dest, banks, live, bank_ref, acc_in, blocks_ref, out_ref, acc_ref):
    acc_ref[...] = acc_in[...]

    def term(j, carry):
        @pl.when(live[j] > 0)
        def _():
            acc_ref[dest[j]] += jnp.dot(
                bank_ref[banks[j]], blocks_ref[j], preferred_element_type=jnp.float32
            )

        return carry

    lax.fori_loop(0, dest.shape[0], term, 0)
    out_ref[...] = acc_ref[...].astype(out_ref.dtype)


def _local(kernel, cols, banks, bank, blocks):
    n, tile, width = blocks.shape
    return pl.pallas_call(
        kernel,
        out_shape=jax.ShapeDtypeStruct((n, tile, width), jnp.float32),
        in_specs=[_SMEM, _SMEM, _VMEM, _VMEM],
        out_specs=_VMEM,
        cost_estimate=_cost(cols.size, tile, 2 * bank.size + 2 * blocks.size + 4 * blocks.size),
    )(cols, banks, bank, blocks)


def _halo(dest, banks, live, bank, acc, blocks):
    n, tile, width = acc.shape
    return pl.pallas_call(
        _halo_kernel,
        out_shape=jax.ShapeDtypeStruct((n, tile, width), jnp.bfloat16),
        in_specs=[_SMEM, _SMEM, _SMEM, _VMEM, _VMEM, _VMEM],
        out_specs=_VMEM,
        scratch_shapes=[pltpu.VMEM((n, tile, width), jnp.float32)],
        cost_estimate=_cost(dest.size, tile, 2 * bank.size + 6 * acc.size + 2 * blocks.size),
    )(dest, banks, live, bank, acc, blocks)


def _dom_sum(x):
    domains = lax.axis_size("dom")
    rows, width = x.shape
    piece = -(-rows // domains)
    y = jnp.pad(x, ((0, piece * domains - rows), (0, 0)))
    z = lax.all_to_all(y.reshape(domains, piece, width), "dom", 0, 0, tiled=True).sum(0)
    z = lax.all_to_all(
        jnp.broadcast_to(z[None], (domains, piece, width)), "dom", 0, 0, tiled=True
    ).reshape(domains * piece, width)
    return z[:rows]


def per_device(
    node_feats,
    weight,
    bias,
    cotangent,
    tile_bank,
    local_cols,
    local_banks,
    published,
    send_table,
    halo_rows,
    halo_banks,
):
    domains = lax.axis_size("dom")
    groups = lax.axis_size("grp")
    domain_index = lax.axis_index("dom")
    rows_here = node_feats.shape[0]
    tile_size = tile_bank.shape[1]
    slot_count = send_table.shape[2]
    features = lax.all_to_all(node_feats, "grp", split_axis=1, concat_axis=0, tiled=True)
    part_rows, narrow = features.shape
    blocks = part_rows // tile_size
    feat_blocks = features.reshape(blocks, tile_size, narrow)
    cols_here = local_cols[0]
    banks_here = local_banks[0]
    own_pub = published[0]
    bank_t = jnp.swapaxes(tile_bank, 1, 2)

    outgoing = lax.dynamic_index_in_dim(send_table, domain_index, 0, keepdims=False)
    send_ids = own_pub[jnp.maximum(outgoing, 0)]
    remote = lax.all_to_all(feat_blocks[send_ids], "dom", 0, 0, tiled=True)
    incoming = lax.dynamic_index_in_dim(send_table, domain_index, 1, keepdims=False)
    live_in = (incoming >= 0).astype(jnp.int32).reshape(-1)
    rows_in = halo_rows[0]

    local_acc = _local(_fwd_local_kernel, cols_here, banks_here, tile_bank, feat_blocks)
    agg_blocks = _halo(
        rows_in.reshape(-1),
        halo_banks[0].reshape(-1),
        live_in,
        tile_bank,
        local_acc,
        remote.reshape(domains * slot_count, tile_size, narrow),
    )
    agg_narrow = agg_blocks.reshape(part_rows, narrow)
    aggregated = lax.all_to_all(agg_narrow, "grp", split_axis=0, concat_axis=1, tiled=True)
    pre_act = jnp.dot(aggregated, weight, preferred_element_type=jnp.float32) + bias
    activations = jnp.maximum(pre_act, 0.0).astype(jnp.bfloat16)
    grad_pre = jnp.where(pre_act > 0, cotangent.astype(jnp.float32), 0.0).astype(jnp.bfloat16)
    grad_full = lax.all_to_all(
        jnp.broadcast_to(grad_pre[None], (groups,) + grad_pre.shape), "grp", 0, 0, tiled=True
    ).reshape(part_rows, grad_pre.shape[1])
    group_index = lax.axis_index("grp")
    weight_rows = lax.dynamic_slice_in_dim(weight, group_index * narrow, narrow, 0)
    grad_narrow = lax.dot_general(
        grad_full, weight_rows, (((1,), (1,)), ((), ())), preferred_element_type=jnp.float32
    ).astype(jnp.bfloat16)
    grad_blocks = grad_narrow.reshape(blocks, tile_size, narrow)
    weight_part = lax.dot_general(
        agg_narrow, grad_full, (((0,), (0,)), ((), ())), preferred_element_type=jnp.float32
    )
    bias_part = jnp.sum(grad_full.astype(jnp.float32), axis=0)

    back_in = lax.all_to_all(grad_blocks[rows_in], "dom", 0, 0, tiled=True)
    all_banks = lax.all_gather(halo_banks[0], "dom", axis=0, tiled=False)
    banks_back = lax.dynamic_index_in_dim(all_banks, domain_index, 1, keepdims=False)
    live_out = (outgoing >= 0).astype(jnp.int32).reshape(-1)

    local_back = _local(_bwd_local_kernel, cols_here, banks_here, bank_t, grad_blocks)
    grad_total = _halo(
        send_ids.reshape(-1),
        banks_back.reshape(-1),
        live_out,
        bank_t,
        local_back,
        back_in.reshape(domains * slot_count, tile_size, narrow),
    )
    grad_nodes = lax.all_to_all(
        grad_total.reshape(part_rows, narrow),
        "grp",
        split_axis=0,
        concat_axis=1,
        tiled=True,
    )
    norm_scale = float(rows_here * groups * domains) ** (-0.5)
    summed = _dom_sum(jnp.concatenate([weight_part, bias_part[None]], axis=0))
    weight_total = lax.all_to_all(
        jnp.broadcast_to(summed[None, :narrow], (groups, narrow, summed.shape[1])),
        "grp",
        0,
        0,
        tiled=True,
    ).reshape(groups * narrow, summed.shape[1])
    return (
        activations,
        grad_nodes,
        weight_total * norm_scale,
        summed[narrow] * norm_scale,
    )


def solution(mesh):
    in_specs = (
        P(("dom", "grp"), None),
        P(),
        P(),
        P(("dom", "grp"), None),
        P(),
        P("dom", None, None),
        P("dom", None, None),
        P("dom", None),
        P(),
        P("dom", None, None),
        P("dom", None, None),
    )
    out_specs = (P(("dom", "grp"), None), P(("dom", "grp"), None), P(), P())
    return jax.shard_map(
        per_device, mesh=mesh, in_specs=in_specs, out_specs=out_specs, check_vma=False
    )
```

```python
import functools

import jax
import jax.numpy as jnp
from jax import lax
from jax.experimental import pallas as pl
from jax.experimental.pallas import tpu as pltpu
from jax.sharding import PartitionSpec as P

_SMEM = pl.BlockSpec(memory_space=pltpu.SMEM)
_VMEM = pl.BlockSpec(memory_space=pltpu.VMEM)


def _cost(matmuls, tile, nbytes):
    return pl.CostEstimate(
        flops=2 * matmuls * tile * tile * tile, transcendentals=0, bytes_accessed=nbytes
    )


def _fwd_local_kernel(cols, banks, bank_ref, feat_ref, acc_ref):
    rows, tiles = cols.shape

    def row(r, carry):
        total = jnp.zeros(acc_ref.shape[1:], jnp.float32)
        for k in range(tiles):
            total += jnp.dot(
                bank_ref[banks[r, k]], feat_ref[cols[r, k]], preferred_element_type=jnp.float32
            )
        acc_ref[r] = total
        return carry

    lax.fori_loop(0, rows, row, 0)


def _bwd_local_kernel(cols, banks, bank_t_ref, grad_ref, acc_ref):
    rows, tiles = cols.shape
    acc_ref[...] = jnp.zeros(acc_ref.shape, jnp.float32)

    def row(r, carry):
        block = grad_ref[r]
        for k in range(tiles):
            c = cols[r, k]
            acc_ref[c] += jnp.dot(
                bank_t_ref[banks[r, k]], block, preferred_element_type=jnp.float32
            )
        return carry

    lax.fori_loop(0, rows, row, 0)


def _halo_kernel(dest, banks, live, bank_ref, acc_in, blocks_ref, out_ref, acc_ref):
    acc_ref[...] = acc_in[...]

    def term(j, carry):
        @pl.when(live[j] > 0)
        def _():
            acc_ref[dest[j]] += jnp.dot(
                bank_ref[banks[j]],
                blocks_ref[j, pl.ds(0, acc_ref.shape[1]), :],
                preferred_element_type=jnp.float32,
            )

        return carry

    lax.fori_loop(0, dest.shape[0], term, 0)
    out_ref[...] = acc_ref[...].astype(out_ref.dtype)


def _local(kernel, cols, banks, bank, blocks):
    n, tile, width = blocks.shape
    return pl.pallas_call(
        kernel,
        out_shape=jax.ShapeDtypeStruct((n, tile, width), jnp.float32),
        in_specs=[_SMEM, _SMEM, _VMEM, _VMEM],
        out_specs=_VMEM,
        cost_estimate=_cost(cols.size, tile, 2 * bank.size + 2 * blocks.size + 4 * blocks.size),
    )(cols, banks, bank, blocks)


def _halo(dest, banks, live, bank, acc, blocks):
    n, tile, width = acc.shape
    return pl.pallas_call(
        _halo_kernel,
        out_shape=jax.ShapeDtypeStruct((n, tile, width), jnp.bfloat16),
        in_specs=[_SMEM, _SMEM, _SMEM, _VMEM, _VMEM, _VMEM],
        out_specs=_VMEM,
        scratch_shapes=[pltpu.VMEM((n, tile, width), jnp.float32)],
        cost_estimate=_cost(dest.size, tile, 2 * bank.size + 6 * acc.size + 2 * blocks.size),
    )(dest, banks, live, bank, acc, blocks)


def _dom_sum(x):
    domains = lax.axis_size("dom")
    rows, width = x.shape
    piece = -(-rows // domains)
    y = jnp.pad(x, ((0, piece * domains - rows), (0, 0)))
    z = lax.all_to_all(y.reshape(domains, piece, width), "dom", 0, 0, tiled=True).sum(0)
    z = lax.all_to_all(
        jnp.broadcast_to(z[None], (domains, piece, width)), "dom", 0, 0, tiled=True
    ).reshape(domains * piece, width)
    return z[:rows]


def per_device(
    node_feats,
    weight,
    bias,
    cotangent,
    tile_bank,
    local_cols,
    local_banks,
    published,
    send_table,
    halo_rows,
    halo_banks,
):
    domains = lax.axis_size("dom")
    groups = lax.axis_size("grp")
    domain_index = lax.axis_index("dom")
    rows_here = node_feats.shape[0]
    tile_size = tile_bank.shape[1]
    slot_count = send_table.shape[2]
    features = lax.all_to_all(node_feats, "grp", split_axis=1, concat_axis=0, tiled=True)
    part_rows, narrow = features.shape
    blocks = part_rows // tile_size
    feat_blocks = features.reshape(blocks, tile_size, narrow)
    cols_here = local_cols[0]
    banks_here = local_banks[0]
    own_pub = published[0]
    bank_t = jnp.swapaxes(tile_bank, 1, 2)

    outgoing = lax.dynamic_index_in_dim(send_table, domain_index, 0, keepdims=False)
    send_ids = own_pub[jnp.maximum(outgoing, 0)]
    remote = lax.all_to_all(feat_blocks[send_ids], "dom", 0, 0, tiled=True)
    incoming = lax.dynamic_index_in_dim(send_table, domain_index, 1, keepdims=False)
    live_in = (incoming >= 0).astype(jnp.int32).reshape(-1)
    rows_in = halo_rows[0]

    local_acc = _local(_fwd_local_kernel, cols_here, banks_here, tile_bank, feat_blocks)
    agg_blocks = _halo(
        rows_in.reshape(-1),
        halo_banks[0].reshape(-1),
        live_in,
        tile_bank,
        local_acc,
        remote.reshape(domains * slot_count, tile_size, narrow),
    )
    agg_narrow = agg_blocks.reshape(part_rows, narrow)
    aggregated = lax.all_to_all(agg_narrow, "grp", split_axis=0, concat_axis=1, tiled=True)
    pre_act = jnp.dot(aggregated, weight, preferred_element_type=jnp.float32) + bias
    activations = jnp.maximum(pre_act, 0.0).astype(jnp.bfloat16)
    grad_pre = jnp.where(pre_act > 0, cotangent.astype(jnp.float32), 0.0).astype(jnp.bfloat16)
    grad_full = lax.all_to_all(
        jnp.broadcast_to(grad_pre[None], (groups,) + grad_pre.shape), "grp", 0, 0, tiled=True
    ).reshape(part_rows, grad_pre.shape[1])
    group_index = lax.axis_index("grp")
    weight_rows = lax.dynamic_slice_in_dim(weight, group_index * narrow, narrow, 0)
    grad_narrow = lax.dot_general(
        grad_full, weight_rows, (((1,), (1,)), ((), ())), preferred_element_type=jnp.float32
    ).astype(jnp.bfloat16)
    grad_blocks = grad_narrow.reshape(blocks, tile_size, narrow)
    weight_part = lax.dot_general(
        agg_narrow, grad_full, (((0,), (0,)), ((), ())), preferred_element_type=jnp.float32
    )
    bias_part = jnp.sum(grad_full.astype(jnp.float32), axis=0)

    bank_rows = jnp.broadcast_to(
        halo_banks[0].astype(jnp.bfloat16)[:, :, None, None], (domains, slot_count, 8, narrow)
    )
    payload = jnp.concatenate([grad_blocks[rows_in], bank_rows], axis=2)
    back_in = lax.all_to_all(payload, "dom", 0, 0, tiled=True)
    banks_back = back_in[:, :, tile_size, 0].astype(jnp.int32)
    live_out = (outgoing >= 0).astype(jnp.int32).reshape(-1)

    local_back = _local(_bwd_local_kernel, cols_here, banks_here, bank_t, grad_blocks)
    grad_total = _halo(
        send_ids.reshape(-1),
        banks_back.reshape(-1),
        live_out,
        bank_t,
        local_back,
        back_in.reshape(domains * slot_count, tile_size + 8, narrow),
    )
    grad_nodes = lax.all_to_all(
        grad_total.reshape(part_rows, narrow),
        "grp",
        split_axis=0,
        concat_axis=1,
        tiled=True,
    )
    norm_scale = float(rows_here * groups * domains) ** (-0.5)
    summed = _dom_sum(jnp.concatenate([weight_part, bias_part[None]], axis=0))
    weight_total = lax.all_to_all(
        jnp.broadcast_to(summed[None, :narrow], (groups, narrow, summed.shape[1])),
        "grp",
        0,
        0,
        tiled=True,
    ).reshape(groups * narrow, summed.shape[1])
    return (
        activations,
        grad_nodes,
        weight_total * norm_scale,
        summed[narrow] * norm_scale,
    )


def solution(mesh):
    in_specs = (
        P(("dom", "grp"), None),
        P(),
        P(),
        P(("dom", "grp"), None),
        P(),
        P("dom", None, None),
        P("dom", None, None),
        P("dom", None),
        P(),
        P("dom", None, None),
        P("dom", None, None),
    )
    out_specs = (P(("dom", "grp"), None), P(("dom", "grp"), None), P(), P())
    return jax.shard_map(
        per_device, mesh=mesh, in_specs=in_specs, out_specs=out_specs, check_vma=False
    )
```

```python
import functools

import jax
import jax.numpy as jnp
from jax import lax
from jax.experimental import pallas as pl
from jax.experimental.pallas import tpu as pltpu
from jax.sharding import PartitionSpec as P

_SMEM = pl.BlockSpec(memory_space=pltpu.SMEM)
_VMEM = pl.BlockSpec(memory_space=pltpu.VMEM)


def _cost(matmuls, tile, nbytes):
    return pl.CostEstimate(
        flops=2 * matmuls * tile * tile * tile, transcendentals=0, bytes_accessed=nbytes
    )


def _fwd_local_kernel(cols, banks, bank_ref, feat_ref, acc_ref):
    rows, tiles = cols.shape

    def row(r, carry):
        total = jnp.zeros(acc_ref.shape[1:], jnp.float32)
        for k in range(tiles):
            total += jnp.dot(
                bank_ref[banks[r, k]], feat_ref[cols[r, k]], preferred_element_type=jnp.float32
            )
        acc_ref[r] = total
        return carry

    lax.fori_loop(0, rows, row, 0)


def _fwd_exchange_kernel(
    domains, cols, banks, bank_ref, feat_ref, send_ref, acc_ref, recv_ref, send_sems, recv_sems, own_sem
):
    me = lax.axis_index("dom")
    group = lax.axis_index("grp")
    mesh_ids = pl.DeviceIdType.MESH

    def remote(target, slot):
        return pltpu.make_async_remote_copy(
            src_ref=send_ref.at[target],
            dst_ref=recv_ref.at[slot],
            send_sem=send_sems.at[target],
            recv_sem=recv_sems.at[slot],
            device_id=(target, group),
            device_id_type=mesh_ids,
        )

    barrier = pltpu.get_barrier_semaphore()

    def greet(i, carry):
        target = lax.rem(me + i, domains)
        pl.semaphore_signal(barrier, 1, device_id=(target, group), device_id_type=mesh_ids)
        return carry

    lax.fori_loop(1, domains, greet, 0)
    pl.semaphore_wait(barrier, domains - 1)

    def send(i, carry):
        remote(lax.rem(me + i, domains), me).start()
        return carry

    lax.fori_loop(1, domains, send, 0)
    own = pltpu.make_async_copy(send_ref.at[me], recv_ref.at[me], own_sem)
    own.start()
    _fwd_local_kernel(cols, banks, bank_ref, feat_ref, acc_ref)
    own.wait()

    def finish(i, carry):
        remote(lax.rem(me + i, domains), me).wait_send()
        remote(me, lax.rem(me + domains - i, domains)).wait_recv()
        return carry

    lax.fori_loop(1, domains, finish, 0)


def _fwd_exchange(cols, banks, bank, blocks, send):
    n, tile, width = blocks.shape
    domains = send.shape[0]
    return pl.pallas_call(
        functools.partial(_fwd_exchange_kernel, domains),
        out_shape=(
            jax.ShapeDtypeStruct((n, tile, width), jnp.float32),
            jax.ShapeDtypeStruct(send.shape, send.dtype),
        ),
        in_specs=[_SMEM, _SMEM, _VMEM, _VMEM, pl.BlockSpec(memory_space=pl.ANY)],
        out_specs=(_VMEM, pl.BlockSpec(memory_space=pl.ANY)),
        scratch_shapes=[
            pltpu.SemaphoreType.DMA((domains,)),
            pltpu.SemaphoreType.DMA((domains,)),
            pltpu.SemaphoreType.DMA,
        ],
        compiler_params=pltpu.CompilerParams(collective_id=0, has_side_effects=True),
        cost_estimate=_cost(cols.size, tile, 2 * bank.size + 6 * blocks.size + 4 * send.size),
    )(cols, banks, bank, blocks, send)


def _bwd_local_kernel(cols, banks, bank_t_ref, grad_ref, acc_ref):
    rows, tiles = cols.shape
    acc_ref[...] = jnp.zeros(acc_ref.shape, jnp.float32)

    def row(r, carry):
        block = grad_ref[r]
        for k in range(tiles):
            c = cols[r, k]
            acc_ref[c] += jnp.dot(
                bank_t_ref[banks[r, k]], block, preferred_element_type=jnp.float32
            )
        return carry

    lax.fori_loop(0, rows, row, 0)


def _halo_kernel(dest, banks, live, bank_ref, acc_in, blocks_ref, out_ref, acc_ref):
    acc_ref[...] = acc_in[...]

    def term(j, carry):
        @pl.when(live[j] > 0)
        def _():
            acc_ref[dest[j]] += jnp.dot(
                bank_ref[banks[j]],
                blocks_ref[j, pl.ds(0, acc_ref.shape[1]), :],
                preferred_element_type=jnp.float32,
            )

        return carry

    lax.fori_loop(0, dest.shape[0], term, 0)
    out_ref[...] = acc_ref[...].astype(out_ref.dtype)


def _local(kernel, cols, banks, bank, blocks):
    n, tile, width = blocks.shape
    return pl.pallas_call(
        kernel,
        out_shape=jax.ShapeDtypeStruct((n, tile, width), jnp.float32),
        in_specs=[_SMEM, _SMEM, _VMEM, _VMEM],
        out_specs=_VMEM,
        cost_estimate=_cost(cols.size, tile, 2 * bank.size + 2 * blocks.size + 4 * blocks.size),
    )(cols, banks, bank, blocks)


def _halo(dest, banks, live, bank, acc, blocks):
    n, tile, width = acc.shape
    return pl.pallas_call(
        _halo_kernel,
        out_shape=jax.ShapeDtypeStruct((n, tile, width), jnp.bfloat16),
        in_specs=[_SMEM, _SMEM, _SMEM, _VMEM, _VMEM, _VMEM],
        out_specs=_VMEM,
        scratch_shapes=[pltpu.VMEM((n, tile, width), jnp.float32)],
        cost_estimate=_cost(dest.size, tile, 2 * bank.size + 6 * acc.size + 2 * blocks.size),
    )(dest, banks, live, bank, acc, blocks)


def _dom_sum(x):
    domains = lax.axis_size("dom")
    rows, width = x.shape
    piece = -(-rows // domains)
    y = jnp.pad(x, ((0, piece * domains - rows), (0, 0)))
    z = lax.all_to_all(y.reshape(domains, piece, width), "dom", 0, 0, tiled=True).sum(0)
    z = lax.all_to_all(
        jnp.broadcast_to(z[None], (domains, piece, width)), "dom", 0, 0, tiled=True
    ).reshape(domains * piece, width)
    return z[:rows]


def per_device(
    node_feats,
    weight,
    bias,
    cotangent,
    tile_bank,
    local_cols,
    local_banks,
    published,
    send_table,
    halo_rows,
    halo_banks,
):
    domains = lax.axis_size("dom")
    groups = lax.axis_size("grp")
    domain_index = lax.axis_index("dom")
    rows_here = node_feats.shape[0]
    tile_size = tile_bank.shape[1]
    slot_count = send_table.shape[2]
    features = lax.all_to_all(node_feats, "grp", split_axis=1, concat_axis=0, tiled=True)
    part_rows, narrow = features.shape
    blocks = part_rows // tile_size
    feat_blocks = features.reshape(blocks, tile_size, narrow)
    cols_here = local_cols[0]
    banks_here = local_banks[0]
    own_pub = published[0]
    bank_t = jnp.swapaxes(tile_bank, 1, 2)

    outgoing = lax.dynamic_index_in_dim(send_table, domain_index, 0, keepdims=False)
    send_ids = own_pub[jnp.maximum(outgoing, 0)]
    incoming = lax.dynamic_index_in_dim(send_table, domain_index, 1, keepdims=False)
    live_in = (incoming >= 0).astype(jnp.int32).reshape(-1)
    rows_in = halo_rows[0]

    local_acc, remote = _fwd_exchange(
        cols_here, banks_here, tile_bank, feat_blocks, feat_blocks[send_ids]
    )
    agg_blocks = _halo(
        rows_in.reshape(-1),
        halo_banks[0].reshape(-1),
        live_in,
        tile_bank,
        local_acc,
        remote.reshape(domains * slot_count, tile_size, narrow),
    )
    agg_narrow = agg_blocks.reshape(part_rows, narrow)
    aggregated = lax.all_to_all(agg_narrow, "grp", split_axis=0, concat_axis=1, tiled=True)
    pre_act = jnp.dot(aggregated, weight, preferred_element_type=jnp.float32) + bias
    activations = jnp.maximum(pre_act, 0.0).astype(jnp.bfloat16)
    grad_pre = jnp.where(pre_act > 0, cotangent.astype(jnp.float32), 0.0).astype(jnp.bfloat16)
    grad_full = lax.all_to_all(
        jnp.broadcast_to(grad_pre[None], (groups,) + grad_pre.shape), "grp", 0, 0, tiled=True
    ).reshape(part_rows, grad_pre.shape[1])
    group_index = lax.axis_index("grp")
    weight_rows = lax.dynamic_slice_in_dim(weight, group_index * narrow, narrow, 0)
    grad_narrow = lax.dot_general(
        grad_full, weight_rows, (((1,), (1,)), ((), ())), preferred_element_type=jnp.float32
    ).astype(jnp.bfloat16)
    grad_blocks = grad_narrow.reshape(blocks, tile_size, narrow)
    weight_part = lax.dot_general(
        agg_narrow, grad_full, (((0,), (0,)), ((), ())), preferred_element_type=jnp.float32
    )
    bias_part = jnp.sum(grad_full.astype(jnp.float32), axis=0)

    bank_rows = jnp.broadcast_to(
        halo_banks[0].astype(jnp.bfloat16)[:, :, None, None], (domains, slot_count, 8, narrow)
    )
    payload = jnp.concatenate([grad_blocks[rows_in], bank_rows], axis=2)
    back_in = lax.all_to_all(payload, "dom", 0, 0, tiled=True)
    banks_back = back_in[:, :, tile_size, 0].astype(jnp.int32)
    live_out = (outgoing >= 0).astype(jnp.int32).reshape(-1)

    local_back = _local(_bwd_local_kernel, cols_here, banks_here, bank_t, grad_blocks)
    grad_total = _halo(
        send_ids.reshape(-1),
        banks_back.reshape(-1),
        live_out,
        bank_t,
        local_back,
        back_in.reshape(domains * slot_count, tile_size + 8, narrow),
    )
    grad_nodes = lax.all_to_all(
        grad_total.reshape(part_rows, narrow),
        "grp",
        split_axis=0,
        concat_axis=1,
        tiled=True,
    )
    norm_scale = float(rows_here * groups * domains) ** (-0.5)
    summed = _dom_sum(jnp.concatenate([weight_part, bias_part[None]], axis=0))
    weight_total = lax.all_to_all(
        jnp.broadcast_to(summed[None, :narrow], (groups, narrow, summed.shape[1])),
        "grp",
        0,
        0,
        tiled=True,
    ).reshape(groups * narrow, summed.shape[1])
    return (
        activations,
        grad_nodes,
        weight_total * norm_scale,
        summed[narrow] * norm_scale,
    )


def solution(mesh):
    in_specs = (
        P(("dom", "grp"), None),
        P(),
        P(),
        P(("dom", "grp"), None),
        P(),
        P("dom", None, None),
        P("dom", None, None),
        P("dom", None),
        P(),
        P("dom", None, None),
        P("dom", None, None),
    )
    out_specs = (P(("dom", "grp"), None), P(("dom", "grp"), None), P(), P())
    return jax.shard_map(
        per_device, mesh=mesh, in_specs=in_specs, out_specs=out_specs, check_vma=False
    )
```

```python
import functools

import jax
import jax.numpy as jnp
from jax import lax
from jax.experimental import pallas as pl
from jax.experimental.pallas import tpu as pltpu
from jax.sharding import PartitionSpec as P

_SMEM = pl.BlockSpec(memory_space=pltpu.SMEM)
_VMEM = pl.BlockSpec(memory_space=pltpu.VMEM)


def _cost(matmuls, tile, nbytes):
    return pl.CostEstimate(
        flops=2 * matmuls * tile * tile * tile, transcendentals=0, bytes_accessed=nbytes
    )


def _fwd_local_kernel(cols, banks, bank_ref, feat_ref, acc_ref):
    rows, tiles = cols.shape

    def row(r, carry):
        total = jnp.zeros(acc_ref.shape[1:], jnp.float32)
        for k in range(tiles):
            total += jnp.dot(
                bank_ref[banks[r, k]], feat_ref[cols[r, k]], preferred_element_type=jnp.float32
            )
        acc_ref[r] = total
        return carry

    lax.fori_loop(0, rows, row, 0)


def _fwd_exchange_kernel(
    domains, cols, banks, bank_ref, feat_ref, send_ref, acc_ref, recv_ref, send_sems, recv_sems, own_sem
):
    me = lax.axis_index("dom")
    group = lax.axis_index("grp")
    mesh_ids = pl.DeviceIdType.MESH

    def remote(target, slot):
        return pltpu.make_async_remote_copy(
            src_ref=send_ref.at[target],
            dst_ref=recv_ref.at[slot],
            send_sem=send_sems.at[target],
            recv_sem=recv_sems.at[slot],
            device_id=(target, group),
            device_id_type=mesh_ids,
        )

    barrier = pltpu.get_barrier_semaphore()

    def greet(i, carry):
        target = lax.rem(me + i, domains)
        pl.semaphore_signal(barrier, 1, device_id=(target, group), device_id_type=mesh_ids)
        return carry

    lax.fori_loop(1, domains, greet, 0)
    pl.semaphore_wait(barrier, domains - 1)

    def send(i, carry):
        remote(lax.rem(me + i, domains), me).start()
        return carry

    lax.fori_loop(1, domains, send, 0)
    own = pltpu.make_async_copy(send_ref.at[me], recv_ref.at[me], own_sem)
    own.start()
    _fwd_local_kernel(cols, banks, bank_ref, feat_ref, acc_ref)
    own.wait()

    def finish(i, carry):
        remote(lax.rem(me + i, domains), me).wait_send()
        remote(me, lax.rem(me + domains - i, domains)).wait_recv()
        return carry

    lax.fori_loop(1, domains, finish, 0)


def _fwd_exchange(cols, banks, bank, blocks, send):
    n, tile, width = blocks.shape
    domains = send.shape[0]
    return pl.pallas_call(
        functools.partial(_fwd_exchange_kernel, domains),
        out_shape=(
            jax.ShapeDtypeStruct((n, tile, width), jnp.float32),
            jax.ShapeDtypeStruct(send.shape, send.dtype),
        ),
        in_specs=[_SMEM, _SMEM, _VMEM, _VMEM, pl.BlockSpec(memory_space=pl.ANY)],
        out_specs=(_VMEM, pl.BlockSpec(memory_space=pl.ANY)),
        scratch_shapes=[
            pltpu.SemaphoreType.DMA((domains,)),
            pltpu.SemaphoreType.DMA((domains,)),
            pltpu.SemaphoreType.DMA,
        ],
        compiler_params=pltpu.CompilerParams(collective_id=0, has_side_effects=True),
        cost_estimate=_cost(cols.size, tile, 2 * bank.size + 6 * blocks.size + 4 * send.size),
    )(cols, banks, bank, blocks, send)


def _bwd_local_kernel(cols, banks, bank_t_ref, grad_ref, acc_ref):
    rows, tiles = cols.shape
    acc_ref[...] = jnp.zeros(acc_ref.shape, jnp.float32)

    def row(r, carry):
        block = grad_ref[r]
        for k in range(tiles):
            c = cols[r, k]
            acc_ref[c] += jnp.dot(
                bank_t_ref[banks[r, k]], block, preferred_element_type=jnp.float32
            )
        return carry

    lax.fori_loop(0, rows, row, 0)


def _halo_kernel(dest, banks, live, bank_ref, acc_in, blocks_ref, out_ref, acc_ref):
    acc_ref[...] = acc_in[...]

    def term(j, carry):
        @pl.when(live[j] > 0)
        def _():
            acc_ref[dest[j]] += jnp.dot(
                bank_ref[banks[j]],
                blocks_ref[j, pl.ds(0, acc_ref.shape[1]), :],
                preferred_element_type=jnp.float32,
            )

        return carry

    lax.fori_loop(0, dest.shape[0], term, 0)
    out_ref[...] = acc_ref[...].astype(out_ref.dtype)


def _local(kernel, cols, banks, bank, blocks):
    n, tile, width = blocks.shape
    return pl.pallas_call(
        kernel,
        out_shape=jax.ShapeDtypeStruct((n, tile, width), jnp.float32),
        in_specs=[_SMEM, _SMEM, _VMEM, _VMEM],
        out_specs=_VMEM,
        cost_estimate=_cost(cols.size, tile, 2 * bank.size + 2 * blocks.size + 4 * blocks.size),
    )(cols, banks, bank, blocks)


def _halo(dest, banks, live, bank, acc, blocks):
    n, tile, width = acc.shape
    return pl.pallas_call(
        _halo_kernel,
        out_shape=jax.ShapeDtypeStruct((n, tile, width), jnp.bfloat16),
        in_specs=[_SMEM, _SMEM, _SMEM, _VMEM, _VMEM, _VMEM],
        out_specs=_VMEM,
        scratch_shapes=[pltpu.VMEM((n, tile, width), jnp.float32)],
        cost_estimate=_cost(dest.size, tile, 2 * bank.size + 6 * acc.size + 2 * blocks.size),
    )(dest, banks, live, bank, acc, blocks)


def _dom_sum(x):
    domains = lax.axis_size("dom")
    rows, width = x.shape
    piece = -(-rows // domains)
    y = jnp.pad(x, ((0, piece * domains - rows), (0, 0)))
    z = lax.all_to_all(y.reshape(domains, piece, width), "dom", 0, 0, tiled=True).sum(0)
    z = lax.all_to_all(
        jnp.broadcast_to(z[None], (domains, piece, width)), "dom", 0, 0, tiled=True
    ).reshape(domains * piece, width)
    return z[:rows]


def per_device(
    node_feats,
    weight,
    bias,
    cotangent,
    tile_bank,
    local_cols,
    local_banks,
    published,
    send_table,
    halo_rows,
    halo_banks,
):
    domains = lax.axis_size("dom")
    groups = lax.axis_size("grp")
    domain_index = lax.axis_index("dom")
    rows_here = node_feats.shape[0]
    tile_size = tile_bank.shape[1]
    slot_count = send_table.shape[2]
    features = lax.all_to_all(node_feats, "grp", split_axis=1, concat_axis=0, tiled=True)
    part_rows, narrow = features.shape
    blocks = part_rows // tile_size
    feat_blocks = features.reshape(blocks, tile_size, narrow)
    cols_here = local_cols[0]
    banks_here = local_banks[0]
    own_pub = published[0]
    bank_t = jnp.swapaxes(tile_bank, 1, 2)

    outgoing = lax.dynamic_index_in_dim(send_table, domain_index, 0, keepdims=False)
    send_ids = own_pub[jnp.maximum(outgoing, 0)]
    incoming = lax.dynamic_index_in_dim(send_table, domain_index, 1, keepdims=False)
    live_in = (incoming >= 0).astype(jnp.int32).reshape(-1)
    rows_in = halo_rows[0]

    local_acc, remote = _fwd_exchange(
        cols_here, banks_here, tile_bank, feat_blocks, feat_blocks[send_ids]
    )
    agg_blocks = _halo(
        rows_in.reshape(-1),
        halo_banks[0].reshape(-1),
        live_in,
        tile_bank,
        local_acc,
        remote.reshape(domains * slot_count, tile_size, narrow),
    )
    agg_narrow = agg_blocks.reshape(part_rows, narrow)
    aggregated = lax.all_to_all(agg_narrow, "grp", split_axis=0, concat_axis=1, tiled=True)
    pre_act = jnp.dot(aggregated, weight, preferred_element_type=jnp.float32) + bias
    activations = jnp.maximum(pre_act, 0.0).astype(jnp.bfloat16)
    grad_pre = jnp.where(pre_act > 0, cotangent.astype(jnp.float32), 0.0).astype(jnp.bfloat16)
    grad_full = lax.all_to_all(
        jnp.broadcast_to(grad_pre[None], (groups,) + grad_pre.shape), "grp", 0, 0, tiled=True
    ).reshape(part_rows, grad_pre.shape[1])
    group_index = lax.axis_index("grp")
    weight_rows = lax.dynamic_slice_in_dim(weight, group_index * narrow, narrow, 0)
    grad_narrow = lax.dot_general(
        grad_full, weight_rows, (((1,), (1,)), ((), ())), preferred_element_type=jnp.float32
    ).astype(jnp.bfloat16)
    grad_blocks = grad_narrow.reshape(blocks, tile_size, narrow)
    weight_part = lax.dot_general(
        agg_narrow, grad_full, (((0,), (0,)), ((), ())), preferred_element_type=jnp.float32
    )
    bias_part = jnp.sum(grad_full.astype(jnp.float32), axis=0)

    bank_rows = jnp.broadcast_to(
        halo_banks[0].astype(jnp.bfloat16)[:, :, None, None], (domains, slot_count, 8, narrow)
    )
    payload = jnp.concatenate([grad_blocks[rows_in], bank_rows], axis=2)
    halo_rows_sent = slot_count * (tile_size + 8)
    partial = jnp.concatenate([weight_part, bias_part[None]], axis=0)
    kept_rows, width = partial.shape
    piece = -(-kept_rows // domains)
    pieces = jnp.pad(partial, ((0, piece * domains - kept_rows), (0, 0))).reshape(
        domains, piece, width
    )
    high = pieces.astype(jnp.bfloat16)
    low = (pieces - high.astype(jnp.float32)).astype(jnp.bfloat16)
    split = jnp.stack([high, low], axis=1).reshape(domains, -1, narrow)
    mixed = jnp.concatenate([payload.reshape(domains, halo_rows_sent, narrow), split], axis=1)
    arrived = lax.all_to_all(mixed, "dom", 0, 0, tiled=True)
    back_in = arrived[:, :halo_rows_sent].reshape(domains, slot_count, tile_size + 8, narrow)
    banks_back = back_in[:, :, tile_size, 0].astype(jnp.int32)
    parts_in = arrived[:, halo_rows_sent:].reshape(domains, 2, piece, width).astype(jnp.float32)
    reduced = (parts_in[:, 0] + parts_in[:, 1]).sum(0)
    live_out = (outgoing >= 0).astype(jnp.int32).reshape(-1)

    local_back = _local(_bwd_local_kernel, cols_here, banks_here, bank_t, grad_blocks)
    grad_total = _halo(
        send_ids.reshape(-1),
        banks_back.reshape(-1),
        live_out,
        bank_t,
        local_back,
        back_in.reshape(domains * slot_count, tile_size + 8, narrow),
    )
    grad_nodes = lax.all_to_all(
        grad_total.reshape(part_rows, narrow),
        "grp",
        split_axis=0,
        concat_axis=1,
        tiled=True,
    )
    norm_scale = float(rows_here * groups * domains) ** (-0.5)
    summed = lax.all_to_all(
        jnp.broadcast_to(reduced[None], (domains, piece, width)), "dom", 0, 0, tiled=True
    ).reshape(domains * piece, width)
    weight_total = lax.all_to_all(
        jnp.broadcast_to(summed[None, :narrow], (groups, narrow, summed.shape[1])),
        "grp",
        0,
        0,
        tiled=True,
    ).reshape(groups * narrow, summed.shape[1])
    return (
        activations,
        grad_nodes,
        weight_total * norm_scale,
        summed[narrow] * norm_scale,
    )


def solution(mesh):
    in_specs = (
        P(("dom", "grp"), None),
        P(),
        P(),
        P(("dom", "grp"), None),
        P(),
        P("dom", None, None),
        P("dom", None, None),
        P("dom", None),
        P(),
        P("dom", None, None),
        P("dom", None, None),
    )
    out_specs = (P(("dom", "grp"), None), P(("dom", "grp"), None), P(), P())
    return jax.shard_map(
        per_device, mesh=mesh, in_specs=in_specs, out_specs=out_specs, check_vma=False
    )
```

```python
import functools

import jax
import jax.numpy as jnp
from jax import lax
from jax.experimental import pallas as pl
from jax.experimental.pallas import tpu as pltpu
from jax.sharding import PartitionSpec as P

_SMEM = pl.BlockSpec(memory_space=pltpu.SMEM)
_VMEM = pl.BlockSpec(memory_space=pltpu.VMEM)


def _cost(matmuls, tile, nbytes):
    return pl.CostEstimate(
        flops=2 * matmuls * tile * tile * tile, transcendentals=0, bytes_accessed=nbytes
    )


def _fwd_local_kernel(cols, banks, bank_ref, feat_ref, acc_ref):
    rows, tiles = cols.shape

    def row(r, carry):
        total = jnp.zeros(acc_ref.shape[1:], jnp.float32)
        for k in range(tiles):
            total += jnp.dot(
                bank_ref[banks[r, k]], feat_ref[cols[r, k]], preferred_element_type=jnp.float32
            )
        acc_ref[r] = total
        return carry

    lax.fori_loop(0, rows, row, 0)


def _fwd_exchange_kernel(
    domains, cols, banks, bank_ref, feat_ref, send_ref, acc_ref, recv_ref, send_sems, recv_sems, own_sem
):
    me = lax.axis_index("dom")
    group = lax.axis_index("grp")
    mesh_ids = pl.DeviceIdType.MESH

    def remote(target, slot):
        return pltpu.make_async_remote_copy(
            src_ref=send_ref.at[target],
            dst_ref=recv_ref.at[slot],
            send_sem=send_sems.at[target],
            recv_sem=recv_sems.at[slot],
            device_id=(target, group),
            device_id_type=mesh_ids,
        )

    barrier = pltpu.get_barrier_semaphore()

    def greet(i, carry):
        target = lax.rem(me + i, domains)
        pl.semaphore_signal(barrier, 1, device_id=(target, group), device_id_type=mesh_ids)
        return carry

    lax.fori_loop(1, domains, greet, 0)
    pl.semaphore_wait(barrier, domains - 1)

    def send(i, carry):
        remote(lax.rem(me + i, domains), me).start()
        return carry

    lax.fori_loop(1, domains, send, 0)
    own = pltpu.make_async_copy(send_ref.at[me], recv_ref.at[me], own_sem)
    own.start()
    _fwd_local_kernel(cols, banks, bank_ref, feat_ref, acc_ref)
    own.wait()

    def finish(i, carry):
        remote(lax.rem(me + i, domains), me).wait_send()
        remote(me, lax.rem(me + domains - i, domains)).wait_recv()
        return carry

    lax.fori_loop(1, domains, finish, 0)


def _fwd_exchange(cols, banks, bank, blocks, send):
    n, tile, width = blocks.shape
    domains = send.shape[0]
    return pl.pallas_call(
        functools.partial(_fwd_exchange_kernel, domains),
        out_shape=(
            jax.ShapeDtypeStruct((n, tile, width), jnp.float32),
            jax.ShapeDtypeStruct(send.shape, send.dtype),
        ),
        in_specs=[_SMEM, _SMEM, _VMEM, _VMEM, pl.BlockSpec(memory_space=pl.ANY)],
        out_specs=(_VMEM, pl.BlockSpec(memory_space=pl.ANY)),
        scratch_shapes=[
            pltpu.SemaphoreType.DMA((domains,)),
            pltpu.SemaphoreType.DMA((domains,)),
            pltpu.SemaphoreType.DMA,
        ],
        compiler_params=pltpu.CompilerParams(collective_id=0, has_side_effects=True),
        cost_estimate=_cost(cols.size, tile, 2 * bank.size + 6 * blocks.size + 4 * send.size),
    )(cols, banks, bank, blocks, send)


def _exchange_kernel(domains, send_ref, recv_ref, send_sems, recv_sems, own_sem):
    me = lax.axis_index("dom")
    group = lax.axis_index("grp")
    mesh_ids = pl.DeviceIdType.MESH

    def remote(target, slot):
        return pltpu.make_async_remote_copy(
            src_ref=send_ref.at[target],
            dst_ref=recv_ref.at[slot],
            send_sem=send_sems.at[target],
            recv_sem=recv_sems.at[slot],
            device_id=(target, group),
            device_id_type=mesh_ids,
        )

    barrier = pltpu.get_barrier_semaphore()

    def greet(i, carry):
        target = lax.rem(me + i, domains)
        pl.semaphore_signal(barrier, 1, device_id=(target, group), device_id_type=mesh_ids)
        return carry

    lax.fori_loop(1, domains, greet, 0)
    pl.semaphore_wait(barrier, domains - 1)

    def send(i, carry):
        remote(lax.rem(me + i, domains), me).start()
        return carry

    lax.fori_loop(1, domains, send, 0)
    own = pltpu.make_async_copy(send_ref.at[me], recv_ref.at[me], own_sem)
    own.start()
    own.wait()

    def finish(i, carry):
        remote(lax.rem(me + i, domains), me).wait_send()
        remote(me, lax.rem(me + domains - i, domains)).wait_recv()
        return carry

    lax.fori_loop(1, domains, finish, 0)


def _exchange(send):
    domains = send.shape[0]
    return pl.pallas_call(
        functools.partial(_exchange_kernel, domains),
        out_shape=jax.ShapeDtypeStruct(send.shape, send.dtype),
        in_specs=[pl.BlockSpec(memory_space=pl.ANY)],
        out_specs=pl.BlockSpec(memory_space=pl.ANY),
        scratch_shapes=[
            pltpu.SemaphoreType.DMA((domains,)),
            pltpu.SemaphoreType.DMA((domains,)),
            pltpu.SemaphoreType.DMA,
        ],
        compiler_params=pltpu.CompilerParams(collective_id=1, has_side_effects=True),
        cost_estimate=pl.CostEstimate(flops=0, transcendentals=0, bytes_accessed=4 * send.size),
    )(send)


def _bwd_local_kernel(cols, banks, bank_t_ref, grad_ref, acc_ref):
    rows, tiles = cols.shape
    acc_ref[...] = jnp.zeros(acc_ref.shape, jnp.float32)

    def row(r, carry):
        block = grad_ref[r]
        for k in range(tiles):
            c = cols[r, k]
            acc_ref[c] += jnp.dot(
                bank_t_ref[banks[r, k]], block, preferred_element_type=jnp.float32
            )
        return carry

    lax.fori_loop(0, rows, row, 0)


def _halo_kernel(dest, banks, live, bank_ref, acc_in, blocks_ref, out_ref, acc_ref):
    acc_ref[...] = acc_in[...]

    def term(j, carry):
        @pl.when(live[j] > 0)
        def _():
            acc_ref[dest[j]] += jnp.dot(
                bank_ref[banks[j]],
                blocks_ref[j, pl.ds(0, acc_ref.shape[1]), :],
                preferred_element_type=jnp.float32,
            )

        return carry

    lax.fori_loop(0, dest.shape[0], term, 0)
    out_ref[...] = acc_ref[...].astype(out_ref.dtype)


def _local(kernel, cols, banks, bank, blocks):
    n, tile, width = blocks.shape
    return pl.pallas_call(
        kernel,
        out_shape=jax.ShapeDtypeStruct((n, tile, width), jnp.float32),
        in_specs=[_SMEM, _SMEM, _VMEM, _VMEM],
        out_specs=_VMEM,
        cost_estimate=_cost(cols.size, tile, 2 * bank.size + 2 * blocks.size + 4 * blocks.size),
    )(cols, banks, bank, blocks)


def _halo(dest, banks, live, bank, acc, blocks):
    n, tile, width = acc.shape
    return pl.pallas_call(
        _halo_kernel,
        out_shape=jax.ShapeDtypeStruct((n, tile, width), jnp.bfloat16),
        in_specs=[_SMEM, _SMEM, _SMEM, _VMEM, _VMEM, _VMEM],
        out_specs=_VMEM,
        scratch_shapes=[pltpu.VMEM((n, tile, width), jnp.float32)],
        cost_estimate=_cost(dest.size, tile, 2 * bank.size + 6 * acc.size + 2 * blocks.size),
    )(dest, banks, live, bank, acc, blocks)


def _dom_sum(x):
    domains = lax.axis_size("dom")
    rows, width = x.shape
    piece = -(-rows // domains)
    y = jnp.pad(x, ((0, piece * domains - rows), (0, 0)))
    z = lax.all_to_all(y.reshape(domains, piece, width), "dom", 0, 0, tiled=True).sum(0)
    z = lax.all_to_all(
        jnp.broadcast_to(z[None], (domains, piece, width)), "dom", 0, 0, tiled=True
    ).reshape(domains * piece, width)
    return z[:rows]


def per_device(
    node_feats,
    weight,
    bias,
    cotangent,
    tile_bank,
    local_cols,
    local_banks,
    published,
    send_table,
    halo_rows,
    halo_banks,
):
    domains = lax.axis_size("dom")
    groups = lax.axis_size("grp")
    domain_index = lax.axis_index("dom")
    rows_here = node_feats.shape[0]
    tile_size = tile_bank.shape[1]
    slot_count = send_table.shape[2]
    features = lax.all_to_all(node_feats, "grp", split_axis=1, concat_axis=0, tiled=True)
    part_rows, narrow = features.shape
    blocks = part_rows // tile_size
    feat_blocks = features.reshape(blocks, tile_size, narrow)
    cols_here = local_cols[0]
    banks_here = local_banks[0]
    own_pub = published[0]
    bank_t = jnp.swapaxes(tile_bank, 1, 2)

    outgoing = lax.dynamic_index_in_dim(send_table, domain_index, 0, keepdims=False)
    send_ids = own_pub[jnp.maximum(outgoing, 0)]
    incoming = lax.dynamic_index_in_dim(send_table, domain_index, 1, keepdims=False)
    live_in = (incoming >= 0).astype(jnp.int32).reshape(-1)
    rows_in = halo_rows[0]

    local_acc, remote = _fwd_exchange(
        cols_here, banks_here, tile_bank, feat_blocks, feat_blocks[send_ids]
    )
    agg_blocks = _halo(
        rows_in.reshape(-1),
        halo_banks[0].reshape(-1),
        live_in,
        tile_bank,
        local_acc,
        remote.reshape(domains * slot_count, tile_size, narrow),
    )
    agg_narrow = agg_blocks.reshape(part_rows, narrow)
    aggregated = lax.all_to_all(agg_narrow, "grp", split_axis=0, concat_axis=1, tiled=True)
    pre_act = jnp.dot(aggregated, weight, preferred_element_type=jnp.float32) + bias
    activations = jnp.maximum(pre_act, 0.0).astype(jnp.bfloat16)
    grad_pre = jnp.where(pre_act > 0, cotangent.astype(jnp.float32), 0.0).astype(jnp.bfloat16)
    grad_full = lax.all_to_all(
        jnp.broadcast_to(grad_pre[None], (groups,) + grad_pre.shape), "grp", 0, 0, tiled=True
    ).reshape(part_rows, grad_pre.shape[1])
    group_index = lax.axis_index("grp")
    weight_rows = lax.dynamic_slice_in_dim(weight, group_index * narrow, narrow, 0)
    grad_narrow = lax.dot_general(
        grad_full, weight_rows, (((1,), (1,)), ((), ())), preferred_element_type=jnp.float32
    ).astype(jnp.bfloat16)
    grad_blocks = grad_narrow.reshape(blocks, tile_size, narrow)
    weight_part = lax.dot_general(
        agg_narrow, grad_full, (((0,), (0,)), ((), ())), preferred_element_type=jnp.float32
    )
    bias_part = jnp.sum(grad_full.astype(jnp.float32), axis=0)

    bank_rows = jnp.broadcast_to(
        halo_banks[0].astype(jnp.bfloat16)[:, :, None, None], (domains, slot_count, 8, narrow)
    )
    payload = jnp.concatenate([grad_blocks[rows_in], bank_rows], axis=2)
    back_in = _exchange(payload)
    banks_back = back_in[:, :, tile_size, 0].astype(jnp.int32)
    live_out = (outgoing >= 0).astype(jnp.int32).reshape(-1)

    local_back = _local(_bwd_local_kernel, cols_here, banks_here, bank_t, grad_blocks)
    grad_total = _halo(
        send_ids.reshape(-1),
        banks_back.reshape(-1),
        live_out,
        bank_t,
        local_back,
        back_in.reshape(domains * slot_count, tile_size + 8, narrow),
    )
    grad_nodes = lax.all_to_all(
        grad_total.reshape(part_rows, narrow),
        "grp",
        split_axis=0,
        concat_axis=1,
        tiled=True,
    )
    norm_scale = float(rows_here * groups * domains) ** (-0.5)
    summed = _dom_sum(jnp.concatenate([weight_part, bias_part[None]], axis=0))
    weight_total = lax.all_to_all(
        jnp.broadcast_to(summed[None, :narrow], (groups, narrow, summed.shape[1])),
        "grp",
        0,
        0,
        tiled=True,
    ).reshape(groups * narrow, summed.shape[1])
    return (
        activations,
        grad_nodes,
        weight_total * norm_scale,
        summed[narrow] * norm_scale,
    )


def solution(mesh):
    in_specs = (
        P(("dom", "grp"), None),
        P(),
        P(),
        P(("dom", "grp"), None),
        P(),
        P("dom", None, None),
        P("dom", None, None),
        P("dom", None),
        P(),
        P("dom", None, None),
        P("dom", None, None),
    )
    out_specs = (P(("dom", "grp"), None), P(("dom", "grp"), None), P(), P())
    return jax.shard_map(
        per_device, mesh=mesh, in_specs=in_specs, out_specs=out_specs, check_vma=False
    )
```

```python
import functools

import jax
import jax.numpy as jnp
from jax import lax
from jax.experimental import pallas as pl
from jax.experimental.pallas import tpu as pltpu
from jax.sharding import PartitionSpec as P

_SMEM = pl.BlockSpec(memory_space=pltpu.SMEM)
_VMEM = pl.BlockSpec(memory_space=pltpu.VMEM)


def _cost(matmuls, tile, nbytes):
    return pl.CostEstimate(
        flops=2 * matmuls * tile * tile * tile, transcendentals=0, bytes_accessed=nbytes
    )


def _fwd_local_kernel(cols, banks, bank_ref, feat_ref, acc_ref):
    rows, tiles = cols.shape

    def row(r, carry):
        total = jnp.zeros(acc_ref.shape[1:], jnp.float32)
        for k in range(tiles):
            total += jnp.dot(
                bank_ref[banks[r, k]], feat_ref[cols[r, k]], preferred_element_type=jnp.float32
            )
        acc_ref[r] = total
        return carry

    lax.fori_loop(0, rows, row, 0)


def _fwd_exchange_kernel(
    domains, cols, banks, bank_ref, feat_ref, send_ref, acc_ref, recv_ref, send_sems, recv_sems, own_sem
):
    me = lax.axis_index("dom")
    group = lax.axis_index("grp")
    mesh_ids = pl.DeviceIdType.MESH

    def remote(target, slot):
        return pltpu.make_async_remote_copy(
            src_ref=send_ref.at[target],
            dst_ref=recv_ref.at[slot],
            send_sem=send_sems.at[target],
            recv_sem=recv_sems.at[slot],
            device_id=(target, group),
            device_id_type=mesh_ids,
        )

    barrier = pltpu.get_barrier_semaphore()

    def greet(i, carry):
        target = lax.rem(me + i, domains)
        pl.semaphore_signal(barrier, 1, device_id=(target, group), device_id_type=mesh_ids)
        return carry

    lax.fori_loop(1, domains, greet, 0)
    pl.semaphore_wait(barrier, domains - 1)

    def send(i, carry):
        remote(lax.rem(me + i, domains), me).start()
        return carry

    lax.fori_loop(1, domains, send, 0)
    own = pltpu.make_async_copy(send_ref.at[me], recv_ref.at[me], own_sem)
    own.start()
    _fwd_local_kernel(cols, banks, bank_ref, feat_ref, acc_ref)
    own.wait()

    def finish(i, carry):
        remote(lax.rem(me + i, domains), me).wait_send()
        remote(me, lax.rem(me + domains - i, domains)).wait_recv()
        return carry

    lax.fori_loop(1, domains, finish, 0)


def _fwd_exchange(cols, banks, bank, blocks, send):
    n, tile, width = blocks.shape
    domains = send.shape[0]
    return pl.pallas_call(
        functools.partial(_fwd_exchange_kernel, domains),
        out_shape=(
            jax.ShapeDtypeStruct((n, tile, width), jnp.float32),
            jax.ShapeDtypeStruct(send.shape, send.dtype),
        ),
        in_specs=[_SMEM, _SMEM, _VMEM, _VMEM, pl.BlockSpec(memory_space=pl.ANY)],
        out_specs=(_VMEM, pl.BlockSpec(memory_space=pl.ANY)),
        scratch_shapes=[
            pltpu.SemaphoreType.DMA((domains,)),
            pltpu.SemaphoreType.DMA((domains,)),
            pltpu.SemaphoreType.DMA,
        ],
        compiler_params=pltpu.CompilerParams(collective_id=0, has_side_effects=True),
        cost_estimate=_cost(cols.size, tile, 2 * bank.size + 6 * blocks.size + 4 * send.size),
    )(cols, banks, bank, blocks, send)


def _bwd_local_kernel(cols, banks, bank_t_ref, grad_ref, acc_ref):
    rows, tiles = cols.shape
    acc_ref[...] = jnp.zeros(acc_ref.shape, jnp.float32)

    def row(r, carry):
        block = grad_ref[r]
        for k in range(tiles):
            c = cols[r, k]
            acc_ref[c] += jnp.dot(
                bank_t_ref[banks[r, k]], block, preferred_element_type=jnp.float32
            )
        return carry

    lax.fori_loop(0, rows, row, 0)


def _halo_kernel(dest, banks, live, bank_ref, acc_in, blocks_ref, out_ref, acc_ref):
    acc_ref[...] = acc_in[...]

    def term(j, carry):
        @pl.when(live[j] > 0)
        def _():
            acc_ref[dest[j]] += jnp.dot(
                bank_ref[banks[j]],
                blocks_ref[j, pl.ds(0, acc_ref.shape[1]), :],
                preferred_element_type=jnp.float32,
            )

        return carry

    lax.fori_loop(0, dest.shape[0], term, 0)
    out_ref[...] = acc_ref[...].astype(out_ref.dtype)


def _local(kernel, cols, banks, bank, blocks):
    n, tile, width = blocks.shape
    return pl.pallas_call(
        kernel,
        out_shape=jax.ShapeDtypeStruct((n, tile, width), jnp.float32),
        in_specs=[_SMEM, _SMEM, _VMEM, _VMEM],
        out_specs=_VMEM,
        cost_estimate=_cost(cols.size, tile, 2 * bank.size + 2 * blocks.size + 4 * blocks.size),
    )(cols, banks, bank, blocks)


def _halo(dest, banks, live, bank, acc, blocks):
    n, tile, width = acc.shape
    return pl.pallas_call(
        _halo_kernel,
        out_shape=jax.ShapeDtypeStruct((n, tile, width), jnp.bfloat16),
        in_specs=[_SMEM, _SMEM, _SMEM, _VMEM, _VMEM, _VMEM],
        out_specs=_VMEM,
        scratch_shapes=[pltpu.VMEM((n, tile, width), jnp.float32)],
        cost_estimate=_cost(dest.size, tile, 2 * bank.size + 6 * acc.size + 2 * blocks.size),
    )(dest, banks, live, bank, acc, blocks)


def _dom_sum(x):
    domains = lax.axis_size("dom")
    rows, width = x.shape
    piece = -(-rows // domains)
    y = jnp.pad(x, ((0, piece * domains - rows), (0, 0)))
    z = lax.all_to_all(y.reshape(domains, piece, width), "dom", 0, 0, tiled=True).sum(0)
    z = lax.all_to_all(
        jnp.broadcast_to(z[None], (domains, piece, width)), "dom", 0, 0, tiled=True
    ).reshape(domains * piece, width)
    return z[:rows]


def per_device(
    node_feats,
    weight,
    bias,
    cotangent,
    tile_bank,
    local_cols,
    local_banks,
    published,
    send_table,
    halo_rows,
    halo_banks,
):
    domains = lax.axis_size("dom")
    groups = lax.axis_size("grp")
    domain_index = lax.axis_index("dom")
    rows_here = node_feats.shape[0]
    tile_size = tile_bank.shape[1]
    slot_count = send_table.shape[2]
    features = lax.all_to_all(node_feats, "grp", split_axis=1, concat_axis=0, tiled=True)
    part_rows, narrow = features.shape
    blocks = part_rows // tile_size
    feat_blocks = features.reshape(blocks, tile_size, narrow)
    cols_here = local_cols[0]
    banks_here = local_banks[0]
    own_pub = published[0]
    bank_t = jnp.swapaxes(tile_bank, 1, 2)

    outgoing = lax.dynamic_index_in_dim(send_table, domain_index, 0, keepdims=False)
    send_ids = own_pub[jnp.maximum(outgoing, 0)]
    incoming = lax.dynamic_index_in_dim(send_table, domain_index, 1, keepdims=False)
    live_in = (incoming >= 0).astype(jnp.int32).reshape(-1)
    rows_in = halo_rows[0]

    local_acc, remote = _fwd_exchange(
        cols_here, banks_here, tile_bank, feat_blocks, feat_blocks[send_ids]
    )
    agg_blocks = _halo(
        rows_in.reshape(-1),
        halo_banks[0].reshape(-1),
        live_in,
        tile_bank,
        local_acc,
        remote.reshape(domains * slot_count, tile_size, narrow),
    )
    agg_narrow = agg_blocks.reshape(part_rows, narrow)
    aggregated = lax.all_to_all(agg_narrow, "grp", split_axis=0, concat_axis=1, tiled=True)
    pre_act = jnp.dot(aggregated, weight, preferred_element_type=jnp.float32) + bias
    activations = jnp.maximum(pre_act, 0.0).astype(jnp.bfloat16)
    grad_pre = jnp.where(pre_act > 0, cotangent.astype(jnp.float32), 0.0).astype(jnp.bfloat16)
    grad_full = lax.all_to_all(
        jnp.broadcast_to(grad_pre[None], (groups,) + grad_pre.shape), "grp", 0, 0, tiled=True
    ).reshape(part_rows, grad_pre.shape[1])
    group_index = lax.axis_index("grp")
    weight_rows = lax.dynamic_slice_in_dim(weight, group_index * narrow, narrow, 0)
    grad_narrow = lax.dot_general(
        grad_full, weight_rows, (((1,), (1,)), ((), ())), preferred_element_type=jnp.float32
    ).astype(jnp.bfloat16)
    grad_blocks = grad_narrow.reshape(blocks, tile_size, narrow)
    weight_part = lax.dot_general(
        agg_narrow, grad_full, (((0,), (0,)), ((), ())), preferred_element_type=jnp.float32
    )
    bias_part = jnp.sum(grad_full.astype(jnp.float32), axis=0)

    bank_rows = jnp.broadcast_to(
        halo_banks[0].astype(jnp.bfloat16)[:, :, None, None], (domains, slot_count, 8, narrow)
    )
    payload = jnp.concatenate([grad_blocks[rows_in], bank_rows], axis=2)
    back_in = lax.all_to_all(payload, "dom", 0, 0, tiled=True)
    banks_back = back_in[:, :, tile_size, 0].astype(jnp.int32)
    live_out = (outgoing >= 0).astype(jnp.int32).reshape(-1)

    local_back = _local(_bwd_local_kernel, cols_here, banks_here, bank_t, grad_blocks)
    grad_total = _halo(
        send_ids.reshape(-1),
        banks_back.reshape(-1),
        live_out,
        bank_t,
        local_back,
        back_in.reshape(domains * slot_count, tile_size + 8, narrow),
    )
    grad_nodes = lax.all_to_all(
        grad_total.reshape(part_rows, narrow),
        "grp",
        split_axis=0,
        concat_axis=1,
        tiled=True,
    )
    norm_scale = float(rows_here * groups * domains) ** (-0.5)
    partial = jnp.concatenate([weight_part, bias_part[None]], axis=0)
    kept_rows, width = partial.shape
    piece = -(-kept_rows // domains)
    padded = jnp.pad(partial, ((0, piece * domains - kept_rows), (0, 0)))
    reduced = lax.all_to_all(
        padded.reshape(domains, piece, width), "dom", 0, 0, tiled=True
    ).sum(0)
    gathered = lax.all_to_all(
        jnp.broadcast_to(reduced[None], (domains * groups, piece, width)),
        ("dom", "grp"),
        0,
        0,
        tiled=True,
    ).reshape(domains, groups, piece, width)
    slices = jnp.swapaxes(gathered, 0, 1).reshape(groups, domains * piece, width)
    weight_total = slices[:, :narrow].reshape(groups * narrow, width)
    return (
        activations,
        grad_nodes,
        weight_total * norm_scale,
        slices[0, narrow] * norm_scale,
    )


def solution(mesh):
    in_specs = (
        P(("dom", "grp"), None),
        P(),
        P(),
        P(("dom", "grp"), None),
        P(),
        P("dom", None, None),
        P("dom", None, None),
        P("dom", None),
        P(),
        P("dom", None, None),
        P("dom", None, None),
    )
    out_specs = (P(("dom", "grp"), None), P(("dom", "grp"), None), P(), P())
    return jax.shard_map(
        per_device, mesh=mesh, in_specs=in_specs, out_specs=out_specs, check_vma=False
    )
```
